256 devices in a mesh: energy: 64 (over z, x, core), mom: 4 (over y).
Axes of the slice: x: 4, y: 4, z: 8, core: 2. Of those that a mesh axis runs over, the one named last changes fastest.
Arguments:
- green_less: float32 [4, 64, 64, 64, 128], P('mom', 'energy'), may hold values from -6 to 6
- couplings: bfloat16 [32, 3, 64, 64], replicated, may hold values from -0.75 to 0.75
- pair_atoms: int32 [64, 2], replicated, may hold values from 0 to 31
- shift_idx: int32 [3], replicated, may hold values from 1 to 4, as said below
- weights: float32 [2, 3, 4], replicated, may hold values from 0.05 to 1
Outputs:
- sigma_less: float32 [4, 64, 64, 64, 128], P('mom', 'energy')
The draws below stay inside these ranges and needn't reach their ends.
Inputs may be any that keep to these rules, and one draw needn't show every extreme that they name: `shift_idx`: one mode's shift is exactly 4 and another's is exactly 1.
All inputs are finite; a program needn't handle non-finite values.
Results may differ from the reference program's by a relative error of at most 0.0003.
Values sent between devices are 32-bit elements; how exact they have to be, the bound alone decides.
No kernel may reach another device: no remote copies, remote signals or barrier semaphores. Data moves between devices by JAX's collectives and lax.ppermute only.
A program may use at most 64 MiB of HBM per device.

```python
import math
import jax
import jax.numpy as jnp
from jax import lax

B = 64
NMODE = 3
SHIFT_MAX = 4
NATOM = 32
NK = 4
NE = 64
P_SIZE = 64


def draw_shift_idx(key, part):
    first_key, second_key = jax.random.split(key)
    values = jax.random.randint(first_key, (NMODE,), 1, SHIFT_MAX + 1)
    ranking = jax.random.permutation(second_key, NMODE)
    values = values.at[ranking[0]].set(SHIFT_MAX)
    values = values.at[ranking[1]].set(1)
    return values.astype(jnp.int32)


def plant(result, stream_key, smallest, top_value):
    longest = result.shape.index(max(result.shape))
    spots = []
    for shift in (0, 1):
        where = [jax.random.randint(jax.random.fold_in(stream_key, axis), (), 0, length) for axis, length in enumerate(result.shape)]
        where[longest] = (where[longest] + shift) % result.shape[longest]
        spots.append(tuple(where))
    return result.at[spots[0]].set(smallest).at[spots[1]].set(top_value)


def block_levels(rng, extent, pieces, least, high):
    loudness, own = 1.0, jax.random.fold_in(rng, 6)
    for dim, shards_of in pieces:
        steps = jnp.exp(jax.random.uniform(jax.random.fold_in(own, dim), (shards_of,), jnp.float32, least / len(pieces), high / len(pieces)))
        loudness = loudness * jnp.repeat(steps, extent[dim] // shards_of).reshape([-1 if axis == dim else 1 for axis in range(len(extent))])
    return loudness


def normal_values(rng, shape, scale, limit, shards=(), kind=jnp.bfloat16):
    loudness = block_levels(rng, shape, shards, -0.22, 0.18) if shards else 1.0
    drawn = jax.random.normal(rng, shape, jnp.float32) * scale * loudness
    return jnp.minimum(jnp.maximum(drawn, -limit), limit).astype(kind)


def setup_inputs(seed: int = 0) -> dict:
    keys = jax.random.split(jax.random.key(seed), 6)
    return {
        "green_less": normal_values(keys[0], (NK, NE, P_SIZE, B, 2 * B), 1.0, 6.0, ((0, 4), (1, 64)), jnp.float32),
        "couplings": normal_values(keys[1], (NATOM, NMODE, B, B), B ** -0.5, 0.75),
        "pair_atoms": plant(jax.random.randint(keys[2], (P_SIZE, 2), 0, NATOM), jax.random.fold_in(keys[2], 1), 0, NATOM - 1).astype(jnp.int32),
        "shift_idx": draw_shift_idx(jax.random.fold_in(keys[5], 71), 0),
        "weights": jnp.clip(jnp.exp(jax.random.uniform(keys[4], (2, NMODE, NK), jnp.float32, math.log(0.05), math.log(1.0))), 0.05, 1.0),
    }


precise = lax.Precision.HIGHEST


def circulant(weights):
    moments = weights.shape[2]
    target_ids = jnp.arange(moments, dtype=jnp.int32)[:, None]
    source_ids = jnp.arange(moments, dtype=jnp.int32)[None, :]
    offset = (target_ids - source_ids) % moments
    selector = (offset[:, :, None] == jnp.arange(moments, dtype=jnp.int32)[None, None, :]).astype(jnp.float32)
    return jnp.einsum("slm,kjm->slkj", weights, selector, precision=precise)


def pair_sigma(green_pair, left_coupling, right_coupling, mixing, shift_idx):
    moments = green_pair.shape[0]
    energies = green_pair.shape[1]
    orbitals = green_pair.shape[2]
    padded = jnp.pad(green_pair, ((0, 0), (SHIFT_MAX, SHIFT_MAX), (0, 0), (0, 0)))
    summed = jnp.zeros(green_pair.shape, jnp.float32)
    for mode_index in range(NMODE):
        shift_now = shift_idx[mode_index]
        below_shift = lax.dynamic_slice_in_dim(padded, (SHIFT_MAX - shift_now).astype(jnp.int32), energies, 1)
        above_shift = lax.dynamic_slice_in_dim(padded, (SHIFT_MAX + shift_now).astype(jnp.int32), energies, 1)
        mixed = jnp.einsum("kj,jeac->keac", mixing[0, mode_index], below_shift, precision=precise)
        mixed = mixed + jnp.einsum("kj,jeac->keac", mixing[1, mode_index], above_shift, precision=precise)
        left_product = jnp.einsum("ab,kebc->keac", left_coupling[mode_index], mixed, precision=precise)
        halves = left_product.reshape(moments, energies, orbitals, 2, orbitals)
        right_product = jnp.einsum("keaqc,dc->keaqd", halves, right_coupling[mode_index], precision=precise)
        summed = summed + right_product.reshape(green_pair.shape)
    return summed


def reference(green_less, couplings, pair_atoms, shift_idx, weights):
    mixing = circulant(weights)
    coupling_table = couplings.astype(jnp.float32)

    def one_pair(pair_index):
        green_pair = lax.dynamic_index_in_dim(green_less, pair_index, 2, keepdims=False)
        left_coupling = coupling_table[pair_atoms[pair_index, 0]]
        right_coupling = coupling_table[pair_atoms[pair_index, 1]]
        return pair_sigma(green_pair, left_coupling, right_coupling, mixing, shift_idx)

    stacked = lax.map(one_pair, jnp.arange(P_SIZE, dtype=jnp.int32))
    return jnp.moveaxis(stacked, 0, 2)
```

```python
import functools

import jax
import jax.numpy as jnp
from jax import lax
from jax.experimental import pallas as pl
from jax.experimental.pallas import tpu as pltpu
from jax.sharding import Mesh
from jax.sharding import PartitionSpec as P

NMODE = 3
HALO = 4
VMEM_BYTES = 16 * 2**20
LIMIT = pltpu.CompilerParams(vmem_limit_bytes=VMEM_BYTES)
GROUP = ("x", "c", "y")


def tables_kernel(atoms, coupling_hbm, left_ref, right_ref, picked, sems):
    pairs = left_ref.shape[0]
    copies = []
    for pair in range(pairs):
        for side in range(2):
            copy = pltpu.make_async_copy(
                coupling_hbm.at[atoms[pair, side]], picked.at[pair, side], sems.at[pair, side]
            )
            copy.start()
            copies.append(copy)
    for copy in copies:
        copy.wait()
    size = picked.shape[-1]
    nothing = jnp.zeros((size, size), jnp.float32)
    for pair in range(pairs):
        lefts = []
        for mode in range(NMODE):
            left = picked[pair, 0, mode].astype(jnp.float32)
            lefts += [left, left]
            turned = picked[pair, 1, mode].astype(jnp.float32).T
            upper = jnp.concatenate([turned, nothing], axis=1)
            lower = jnp.concatenate([nothing, turned], axis=1)
            both = jnp.concatenate([upper, lower], axis=0).astype(jnp.bfloat16)
            right_ref[pair, mode, 0] = both
            right_ref[pair, mode, 1] = both
        left_ref[pair] = jnp.concatenate(lefts, axis=1).astype(jnp.bfloat16)


def tables(atoms, couplings):
    pairs, size = atoms.shape[0], couplings.shape[-1]
    return pl.pallas_call(
        tables_kernel,
        grid_spec=pltpu.PrefetchScalarGridSpec(
            num_scalar_prefetch=1,
            grid=(1,),
            in_specs=[pl.BlockSpec(memory_space=pl.ANY)],
            out_specs=[
                pl.BlockSpec((pairs, size, 2 * NMODE * size), lambda i, a: (0, 0, 0)),
                pl.BlockSpec((pairs, NMODE, 2, 2 * size, 2 * size), lambda i, a: (0, 0, 0, 0, 0)),
            ],
            scratch_shapes=[
                pltpu.VMEM((pairs, 2, NMODE, size, size), jnp.bfloat16),
                pltpu.SemaphoreType.DMA((pairs, 2)),
            ],
        ),
        out_shape=[
            jax.ShapeDtypeStruct((pairs, size, 2 * NMODE * size), jnp.bfloat16),
            jax.ShapeDtypeStruct((pairs, NMODE, 2, 2 * size, 2 * size), jnp.bfloat16),
        ],
        compiler_params=LIMIT,
        cost_estimate=pl.CostEstimate(flops=1000000, bytes_accessed=4000000, transcendentals=0),
        name="tables",
    )(atoms, couplings)


def fold_kernel(block_ref, low_ref, high_ref):
    half = low_ref.shape[0]
    for energy in range(2 * half):
        target = low_ref if energy < half else high_ref
        first, second, third, fourth = (block_ref[energy, moment] for moment in range(4))
        even, odd = first + third, second + fourth
        target[energy % half, 0] = even + odd
        target[energy % half, 1] = even - odd
        target[energy % half, 2] = first - third
        target[energy % half, 3] = second - fourth


def fold(block, pair):
    energies, moments, _, rows, columns = block.shape
    half = (energies // 2, moments, rows, columns)
    vmem = pl.BlockSpec(half, lambda i: (0, 0, 0, 0))
    return pl.pallas_call(
        fold_kernel,
        grid=(1,),
        in_specs=[
            pl.BlockSpec((energies, moments, None, rows, columns), lambda i: (0, 0, pair, 0, 0))
        ],
        out_specs=[vmem, vmem],
        out_shape=[jax.ShapeDtypeStruct(half, jnp.float32)] * 2,
        compiler_params=LIMIT,
        cost_estimate=pl.CostEstimate(flops=1000000, bytes_accessed=4000000, transcendentals=0),
        name="fold",
    )(block)


def mix_kernel(shifts, weights, below, low, high, above, left_ref, right_ref, *rest):
    out_ref, window, sems = rest[-3:]
    quarter = low.shape[0]
    copies = [
        pltpu.make_async_copy(part, window.at[pl.ds(place * quarter, quarter)], sems.at[place])
        for place, part in enumerate((below, low, high, above))
    ]
    for copy in copies:
        copy.start()
    factors = []
    for mode in range(NMODE):
        for side in range(2):
            w0, w1, w2, w3 = (weights[side, mode, moment] for moment in range(4))
            even, odd = w0 + w2, w1 + w3
            factors.append(
                ((even + odd) * 0.25, (even - odd) * 0.25, (w0 - w2) * 0.5, (w1 - w3) * 0.5)
            )
    for copy in copies:
        copy.wait()
    rows = window.shape[2]

    def one_energy(energy, carry):
        stacked = [[] for _ in range(4)]
        for mode in range(NMODE):
            shift = shifts[mode]
            parts = []
            for side, place in ((0, energy + HALO - shift), (1, energy + HALO + shift)):
                p, q, r, s = factors[2 * mode + side]
                total, swing, d0, d1 = (window[place, part] for part in range(4))
                parts.append((p * total, q * swing, r * d0 - s * d1, s * d0 + r * d1))
            mixed = jnp.concatenate([a + b for a, b in zip(*parts)], axis=0)
            coarse = mixed.astype(jnp.bfloat16)
            fine = (mixed - coarse.astype(jnp.float32)).astype(jnp.bfloat16)
            right = right_ref[mode].reshape(2 * right_ref.shape[2], right_ref.shape[3])
            product = jnp.dot(
                jnp.concatenate([coarse, fine], axis=1), right, preferred_element_type=jnp.float32
            )
            coarse = product.astype(jnp.bfloat16)
            fine = (product - coarse.astype(jnp.float32)).astype(jnp.bfloat16)
            for part in range(4):
                block = slice(part * rows, (part + 1) * rows)
                stacked[part] += [coarse[block], fine[block]]
        columns = jnp.concatenate([jnp.concatenate(pieces, axis=0) for pieces in stacked], axis=1)
        total = jnp.dot(left_ref[...], columns, preferred_element_type=jnp.float32)
        width = out_ref.shape[3]
        plain, swing, v0, v1 = (total[:, part * width : (part + 1) * width] for part in range(4))
        even, odd = plain + swing, plain - swing
        out_ref[energy, 0] = even + v0
        out_ref[energy, 1] = odd + v1
        out_ref[energy, 2] = even - v0
        out_ref[energy, 3] = odd - v1
        return carry

    lax.fori_loop(0, out_ref.shape[0], one_energy, 0, unroll=4)


def mix(shifts, weights, below, low, high, above, left, right, pair, pairs, into=None):
    quarter, moments, rows, columns = low.shape
    shape = (2 * quarter, moments, pairs, rows, columns)
    hbm = pl.BlockSpec(memory_space=pl.ANY)
    smem = pl.BlockSpec(memory_space=pltpu.SMEM)
    held = [] if into is None else [into]
    return pl.pallas_call(
        mix_kernel,
        grid=(1,),
        in_specs=[
            smem,
            smem,
            hbm,
            hbm,
            hbm,
            hbm,
            pl.BlockSpec((None, *left.shape[1:]), lambda i: (pair, 0, 0)),
            pl.BlockSpec((None, *right.shape[1:]), lambda i: (pair, 0, 0, 0, 0)),
            *(hbm for _ in held),
        ],
        out_specs=pl.BlockSpec(
            (2 * quarter, moments, None, rows, columns), lambda i: (0, 0, pair, 0, 0)
        ),
        out_shape=jax.ShapeDtypeStruct(shape, jnp.float32),
        scratch_shapes=[
            pltpu.VMEM((4 * quarter, *low.shape[1:]), jnp.float32),
            pltpu.SemaphoreType.DMA((4,)),
        ],
        input_output_aliases={8: 0} if held else {},
        compiler_params=LIMIT,
        cost_estimate=pl.CostEstimate(flops=5000000000, bytes_accessed=4000000, transcendentals=0),
        name="mix",
    )(shifts, weights, below, low, high, above, left, right, *held)


def on_device(green_less, couplings, pair_atoms, shift_idx, weights):
    pairs, rows, columns = green_less.shape[2:]
    group = lax.axis_size(GROUP)
    moments = lax.axis_size("y")
    planes = lax.axis_size("z")
    here = lax.axis_index(GROUP)
    up = [(plane, plane + 1) for plane in range(planes - 1)]
    down = [(plane + 1, plane) for plane in range(planes - 1)]
    owned = pairs // group
    atoms = lax.dynamic_slice_in_dim(pair_atoms, here * owned, owned, 0)
    left, right = tables(atoms, couplings)
    moved = lax.all_to_all(
        green_less.reshape(group, owned, rows, columns), GROUP, 0, 0, tiled=True
    )
    block = moved.reshape(group // moments, moments, owned, rows, columns)
    halves = []
    for pair in range(owned):
        low, high = fold(block, pair)
        halves.append((lax.ppermute(high, "z", up), low, high, lax.ppermute(low, "z", down)))
    result = None
    for pair in range(owned):
        result = mix(shift_idx, weights, *halves[pair], left, right, pair, owned, result)
    back = lax.all_to_all(
        result.reshape(group, owned, rows, columns), GROUP, 0, 0, tiled=True
    )
    return back.reshape(green_less.shape)


def solution(mesh):
    sizes = dict(mesh.shape)
    chips = sizes["energy"] // 8
    split = Mesh(
        mesh.devices.reshape(chips, 4, 2, sizes["mom"]), ("z", "x", "c", "y")
    )
    placed = P("y", ("z", "x", "c"), None, None, None)

    def step(*args):
        return jax.shard_map(
            on_device,
            mesh=split,
            in_specs=(placed, P(), P(), P(), P()),
            out_specs=placed,
            check_vma=False,
        )(*args)

    return step
```

```python
import functools
import itertools

import jax
import jax.numpy as jnp
from jax import lax
from jax.experimental import pallas as pl
from jax.experimental.pallas import tpu as pltpu
from jax.sharding import Mesh
from jax.sharding import PartitionSpec as P

NMODE = 3
VMEM_BYTES = 16 * 2**20
LIMIT = pltpu.CompilerParams(vmem_limit_bytes=VMEM_BYTES)
GROUP = ("x", "c", "y")
AXES = ("z", "x", "c", "y")


def tables_kernel(atoms, coupling_hbm, left_ref, right_ref, picked, sems):
    pairs = left_ref.shape[0]
    copies = []
    for pair in range(pairs):
        for side in range(2):
            copy = pltpu.make_async_copy(
                coupling_hbm.at[atoms[pair, side]], picked.at[pair, side], sems.at[pair, side]
            )
            copy.start()
            copies.append(copy)
    for copy in copies:
        copy.wait()
    size = picked.shape[-1]
    nothing = jnp.zeros((size, size), jnp.float32)
    for pair in range(pairs):
        lefts = []
        for mode in range(NMODE):
            left = picked[pair, 0, mode].astype(jnp.float32)
            lefts += [left, left]
            turned = picked[pair, 1, mode].astype(jnp.float32).T
            upper = jnp.concatenate([turned, nothing], axis=1)
            lower = jnp.concatenate([nothing, turned], axis=1)
            both = jnp.concatenate([upper, lower], axis=0).astype(jnp.bfloat16)
            right_ref[pair, mode, 0] = both
            right_ref[pair, mode, 1] = both
        left_ref[pair] = jnp.concatenate(lefts, axis=1).astype(jnp.bfloat16)


def tables(atoms, couplings):
    pairs, size = atoms.shape[0], couplings.shape[-1]
    return pl.pallas_call(
        tables_kernel,
        grid_spec=pltpu.PrefetchScalarGridSpec(
            num_scalar_prefetch=1,
            grid=(1,),
            in_specs=[pl.BlockSpec(memory_space=pl.ANY)],
            out_specs=[
                pl.BlockSpec((pairs, size, 2 * NMODE * size), lambda i, a: (0, 0, 0)),
                pl.BlockSpec((pairs, NMODE, 2, 2 * size, 2 * size), lambda i, a: (0, 0, 0, 0, 0)),
            ],
            scratch_shapes=[
                pltpu.VMEM((pairs, 2, NMODE, size, size), jnp.bfloat16),
                pltpu.SemaphoreType.DMA((pairs, 2)),
            ],
        ),
        out_shape=[
            jax.ShapeDtypeStruct((pairs, size, 2 * NMODE * size), jnp.bfloat16),
            jax.ShapeDtypeStruct((pairs, NMODE, 2, 2 * size, 2 * size), jnp.bfloat16),
        ],
        compiler_params=LIMIT,
        cost_estimate=pl.CostEstimate(flops=1000000, bytes_accessed=4000000, transcendentals=0),
        name="tables",
    )(atoms, couplings)


def fold_kernel(block_ref, low_ref, high_ref):
    half = low_ref.shape[0]
    for energy in range(2 * half):
        target = low_ref if energy < half else high_ref
        first, second, third, fourth = (block_ref[energy, moment] for moment in range(4))
        even, odd = first + third, second + fourth
        target[energy % half, 0] = even + odd
        target[energy % half, 1] = even - odd
        target[energy % half, 2] = first - third
        target[energy % half, 3] = second - fourth


def fold(block, pair):
    energies, moments, _, rows, columns = block.shape
    half = (energies // 2, moments, rows, columns)
    vmem = pl.BlockSpec(half, lambda i: (0, 0, 0, 0))
    return pl.pallas_call(
        fold_kernel,
        grid=(1,),
        in_specs=[
            pl.BlockSpec((energies, moments, None, rows, columns), lambda i: (0, 0, pair, 0, 0))
        ],
        out_specs=[vmem, vmem],
        out_shape=[jax.ShapeDtypeStruct(half, jnp.float32)] * 2,
        compiler_params=LIMIT,
        cost_estimate=pl.CostEstimate(flops=1000000, bytes_accessed=4000000, transcendentals=0),
        name="fold",
    )(block)


def mix_kernel(split, place, shifts, weights, first_ref, second_ref, third_ref, left_ref, right_ref, *rest):
    if split:
        kept_ref, away_ref, window, out_ref = rest[-4:]
    else:
        out_ref, window = rest[-2:]
    quarter = first_ref.shape[0]
    for spot, part in enumerate((first_ref, second_ref, third_ref)):
        for energy in range(quarter):
            window[spot * quarter + energy] = part[energy]
    factors = []
    for mode in range(NMODE):
        for side in range(2):
            w0, w1, w2, w3 = (weights[side, mode, moment] for moment in range(4))
            even, odd = w0 + w2, w1 + w3
            factors.append(
                ((even + odd) * 0.25, (even - odd) * 0.25, (w0 - w2) * 0.5, (w1 - w3) * 0.5)
            )
    rows = window.shape[2]

    def one_energy(energy, carry):
        stacked = [[] for _ in range(4)]
        for mode in range(NMODE):
            shift = shifts[mode]
            parts = []
            for side, spot in ((0, energy + quarter - shift), (1, energy + quarter + shift)):
                p, q, r, s = factors[2 * mode + side]
                total, swing, d0, d1 = (window[spot, part] for part in range(4))
                parts.append((p * total, q * swing, r * d0 - s * d1, s * d0 + r * d1))
            mixed = jnp.concatenate([a + b for a, b in zip(*parts)], axis=0)
            coarse = mixed.astype(jnp.bfloat16)
            fine = (mixed - coarse.astype(jnp.float32)).astype(jnp.bfloat16)
            right = right_ref[mode].reshape(2 * right_ref.shape[2], right_ref.shape[3])
            product = jnp.dot(
                jnp.concatenate([coarse, fine], axis=1), right, preferred_element_type=jnp.float32
            )
            coarse = product.astype(jnp.bfloat16)
            fine = (product - coarse.astype(jnp.float32)).astype(jnp.bfloat16)
            for part in range(4):
                block = slice(part * rows, (part + 1) * rows)
                stacked[part] += [coarse[block], fine[block]]
        columns = jnp.concatenate([jnp.concatenate(pieces, axis=0) for pieces in stacked], axis=1)
        total = jnp.dot(left_ref[...], columns, preferred_element_type=jnp.float32)
        width = out_ref.shape[-1]
        plain, swing, v0, v1 = (total[:, part * width : (part + 1) * width] for part in range(4))
        even, odd = plain + swing, plain - swing
        for moment, value in enumerate((even + v0, odd + v1, even - v0, odd - v1)):
            if split:
                away = jnp.where(lax.rem(energy, 2) == place[0], 0, 1)
                out_ref[away, energy // 2, moment] = value
            else:
                out_ref[energy, moment] = value
        return carry

    lax.fori_loop(0, quarter, one_energy, 0, unroll=4)
    if split:
        for x in range(kept_ref.shape[0]):
            kept_ref[x] = out_ref[0, x]
            away_ref[x] = out_ref[1, x]


def mix(split, upper, place, shifts, weights, quarters, left, right, pair, into):
    quarter, moments, rows, columns = quarters[0].shape
    block = (quarter // 2 if split else quarter, moments, rows, columns)
    shape = block if split else (2 * block[0], *block[1:])
    outs = 2 if split else 1
    vmem = pl.BlockSpec(memory_space=pltpu.VMEM)
    smem = pl.BlockSpec(memory_space=pltpu.SMEM)
    scratch = [pltpu.VMEM((3 * quarter, *quarters[0].shape[1:]), jnp.float32)]
    if split:
        scratch.append(pltpu.VMEM((2, *block), jnp.float32))
    return pl.pallas_call(
        functools.partial(mix_kernel, split),
        grid=(1,),
        in_specs=[
            smem,
            smem,
            smem,
            vmem,
            vmem,
            vmem,
            pl.BlockSpec((None, *left.shape[1:]), lambda i: (pair, 0, 0)),
            pl.BlockSpec((None, *right.shape[1:]), lambda i: (pair, 0, 0, 0, 0)),
            *(pl.BlockSpec(memory_space=pl.ANY) for _ in into),
        ],
        out_specs=[pl.BlockSpec(block, lambda i: (0 if split else upper, 0, 0, 0))] * outs,
        out_shape=[jax.ShapeDtypeStruct(shape, jnp.float32)] * outs,
        scratch_shapes=scratch,
        input_output_aliases={8 + index: index for index in range(len(into))},
        compiler_params=LIMIT,
        cost_estimate=pl.CostEstimate(flops=2500000000, bytes_accessed=2000000, transcendentals=0),
        name="mix",
    )(place, shifts, weights, *quarters, left, right, *into)


def sort_kernel(place, kept_low, kept_high, received_low, received_high, *targets):
    core, first = place[0], place[1]
    half = kept_low.shape[0]
    whole = targets[-1]
    targets = targets[:-1]
    for side, pieces in enumerate(((kept_low, kept_high), (received_low, received_high))):
        for x in range(2 * half):
            whole[side, x] = pieces[x // half][x % half]
    for step, target in enumerate(targets):
        where = lax.rem(first + step, 4)
        for other in range(4):
            x = jnp.where(core == 0, other, where)
            moment = jnp.where(core == 0, where, other)
            target[core, other] = whole[0, x, moment]
            target[1 - core, other] = whole[1, x, moment]


def turn_kernel(place, *refs):
    sources, targets = refs[:4], refs[4:]
    for step, target in enumerate(targets):
        column = lax.rem(place[2] + step, 4)
        for behind, source in enumerate(sources):
            for owner in range(2):
                target[behind, owner] = source[owner, column]


def move(kernel, place, arrays, shape, scratch=()):
    vmem = pl.BlockSpec(memory_space=pltpu.VMEM)
    return list(
        pl.pallas_call(
            kernel,
            in_specs=[pl.BlockSpec(memory_space=pltpu.SMEM)] + [vmem] * len(arrays),
            out_specs=[vmem] * 4,
            out_shape=[jax.ShapeDtypeStruct(shape, jnp.float32)] * 4,
            scratch_shapes=scratch,
            compiler_params=LIMIT,
            cost_estimate=pl.CostEstimate(flops=1000000, bytes_accessed=2000000, transcendentals=0),
        )(place, *arrays)
    )


def place_kernel(place, held, *rest):
    sources, (out, sems) = rest[:4], rest[4:]
    core, first, second = place[0], place[1], place[2]
    copies = []
    for step, source in enumerate(sources):
        along_second = lax.rem(second + 4 - step, 4)
        for behind in range(4):
            along_first = lax.rem(first + 4 - behind, 4)
            x = jnp.where(core == 0, along_second, along_first)
            y = jnp.where(core == 0, along_first, along_second)
            for owner in range(2):
                pair = x * 8 + owner * 4 + y
                copies.append(
                    pltpu.make_async_copy(
                        source.at[behind, owner], out.at[pair, 0], sems.at[step, behind, owner]
                    )
                )
    for copy in copies:
        copy.start()
    for copy in copies:
        copy.wait()


def fill_kernel(back, out, sem):
    copy = pltpu.make_async_copy(back, out.at[:, 1], sem.at[0])
    copy.start()
    copy.wait()


def put(place, landed, back):
    group, rows, columns = back.shape
    hbm = pl.BlockSpec(memory_space=pl.ANY)
    result = jax.ShapeDtypeStruct((group, 2, rows, columns), jnp.float32)
    cost = pl.CostEstimate(flops=1000000, bytes_accessed=4000000, transcendentals=0)
    half = pl.pallas_call(
        fill_kernel,
        in_specs=[hbm],
        out_specs=hbm,
        out_shape=result,
        scratch_shapes=[pltpu.SemaphoreType.DMA((1,))],
        compiler_params=LIMIT,
        cost_estimate=cost,
        name="fill",
    )(back)
    return pl.pallas_call(
        place_kernel,
        in_specs=[pl.BlockSpec(memory_space=pltpu.SMEM)] + [hbm] * 5,
        out_specs=hbm,
        out_shape=result,
        scratch_shapes=[pltpu.SemaphoreType.DMA((4, 4, 2))],
        input_output_aliases={1: 0},
        compiler_params=LIMIT,
        cost_estimate=cost,
        name="place",
    )(place, half, *landed)


def ring(fn):
    sizes = [lax.axis_size(axis) for axis in AXES]
    pairs = []
    for z, x, c, y in itertools.product(*map(range, sizes)):
        tx, tc, ty = fn(x, c, y)
        pairs.append((((z * sizes[1] + x) * sizes[2] + c) * sizes[3] + y,
                      ((z * sizes[1] + tx % 4) * sizes[2] + tc) * sizes[3] + ty % 4))
    return pairs


def along(step, core):
    return ring(lambda x, c, y: (x, c, y + step) if c == core else (x + step, c, y))


def on_device(green_less, couplings, pair_atoms, shift_idx, weights):
    pairs, rows, columns = green_less.shape[2:]
    group = lax.axis_size(GROUP)
    moments = lax.axis_size("y")
    planes = lax.axis_size("z")
    here = lax.axis_index(GROUP)
    up = [(plane, plane + 1) for plane in range(planes - 1)]
    down = [(plane + 1, plane) for plane in range(planes - 1)]
    owned = pairs // group
    atoms = lax.dynamic_slice_in_dim(pair_atoms, here * owned, owned, 0)
    couplings = pltpu.with_memory_space_constraint(couplings, pltpu.HBM)
    x, c, y = (lax.axis_index(axis) for axis in GROUP)
    first, second = jnp.where(c == 0, y, x), jnp.where(c == 0, x, y)
    place = jnp.stack([c, first, second]).astype(jnp.int32)
    left, right = tables(atoms, couplings)
    moved = lax.all_to_all(
        green_less.reshape(group, owned, rows, columns), GROUP, 0, 0, tiled=True
    )
    block = moved.reshape(group // moments, moments, owned, rows, columns)
    halves = []
    for pair in range(owned):
        low, high = fold(block, pair)
        below = lax.ppermute(high, "z", up)
        above = lax.ppermute(low, "z", down)
        halves.append((below, low, high, above))

    def compute(split, upper, pair, into=()):
        quarters = halves[pair][upper : upper + 3]
        return mix(split, upper, place, shift_idx, weights, quarters, left, right, pair, into)

    kept, received = [], []
    for upper in range(2):
        stay, away = compute(True, upper, 0)
        received.append(lax.ppermute(away, AXES, ring(lambda x, c, y: (x, 1 - c, y))))
        kept.append(stay)
    arrived = move(
        sort_kernel,
        place,
        (*kept, *received),
        (2, 4, rows, columns),
        [pltpu.VMEM((2, 4, 4, rows, columns), jnp.float32)],
    )
    for step in (2, 1, 3):
        arrived[step] = lax.ppermute(arrived[step], AXES, along(step, 0))
    (result,) = compute(False, 1, 1, compute(False, 0, 1))
    back = lax.all_to_all(result.reshape(group, rows, columns), GROUP, 0, 0, tiled=True)
    landed = move(turn_kernel, place, arrived, (4, 2, rows, columns))
    for step in (2, 1, 3):
        landed[step] = lax.ppermute(landed[step], AXES, along(step, 1))
    return put(place, landed, back).reshape(green_less.shape)


def solution(mesh):
    sizes = dict(mesh.shape)
    chips = sizes["energy"] // 8
    split = Mesh(
        mesh.devices.reshape(chips, 4, 2, sizes["mom"]), ("z", "x", "c", "y")
    )
    placed = P("y", ("z", "x", "c"), None, None, None)

    return jax.shard_map(
        on_device,
        mesh=split,
        in_specs=(placed, P(), P(), P(), P()),
        out_specs=placed,
        check_vma=False,
    )
```

```python
import functools
import itertools

import jax
import jax.numpy as jnp
from jax import lax
from jax.experimental import pallas as pl
from jax.experimental.pallas import tpu as pltpu
from jax.sharding import Mesh
from jax.sharding import PartitionSpec as P

NMODE = 3
VMEM_BYTES = 16 * 2**20
LIMIT = pltpu.CompilerParams(vmem_limit_bytes=VMEM_BYTES)
GROUP = ("x", "c", "y")
AXES = ("z", "x", "c", "y")


def tables_kernel(atoms, coupling_hbm, left_ref, right_ref, picked, sems):
    pairs = left_ref.shape[0]
    copies = []
    for pair in range(pairs):
        for side in range(2):
            copy = pltpu.make_async_copy(
                coupling_hbm.at[atoms[pair, side]], picked.at[pair, side], sems.at[pair, side]
            )
            copy.start()
            copies.append(copy)
    for copy in copies:
        copy.wait()
    size = picked.shape[-1]
    nothing = jnp.zeros((size, size), jnp.float32)
    for pair in range(pairs):
        lefts = []
        for mode in range(NMODE):
            left = picked[pair, 0, mode].astype(jnp.float32)
            lefts += [left, left]
            turned = picked[pair, 1, mode].astype(jnp.float32).T
            upper = jnp.concatenate([turned, nothing], axis=1)
            lower = jnp.concatenate([nothing, turned], axis=1)
            both = jnp.concatenate([upper, lower], axis=0).astype(jnp.bfloat16)
            right_ref[pair, mode, 0] = both
            right_ref[pair, mode, 1] = both
        left_ref[pair] = jnp.concatenate(lefts, axis=1).astype(jnp.bfloat16)


def tables(atoms, couplings):
    pairs, size = atoms.shape[0], couplings.shape[-1]
    return pl.pallas_call(
        tables_kernel,
        grid_spec=pltpu.PrefetchScalarGridSpec(
            num_scalar_prefetch=1,
            grid=(1,),
            in_specs=[pl.BlockSpec(memory_space=pl.ANY)],
            out_specs=[
                pl.BlockSpec((pairs, size, 2 * NMODE * size), lambda i, a: (0, 0, 0)),
                pl.BlockSpec((pairs, NMODE, 2, 2 * size, 2 * size), lambda i, a: (0, 0, 0, 0, 0)),
            ],
            scratch_shapes=[
                pltpu.VMEM((pairs, 2, NMODE, size, size), jnp.bfloat16),
                pltpu.SemaphoreType.DMA((pairs, 2)),
            ],
        ),
        out_shape=[
            jax.ShapeDtypeStruct((pairs, size, 2 * NMODE * size), jnp.bfloat16),
            jax.ShapeDtypeStruct((pairs, NMODE, 2, 2 * size, 2 * size), jnp.bfloat16),
        ],
        compiler_params=LIMIT,
        cost_estimate=pl.CostEstimate(flops=1000000, bytes_accessed=4000000, transcendentals=0),
        name="tables",
    )(atoms, couplings)


def fold_kernel(block_ref, low_ref, high_ref):
    half = low_ref.shape[0]
    for energy in range(2 * half):
        target = low_ref if energy < half else high_ref
        first, second, third, fourth = (block_ref[energy, moment] for moment in range(4))
        even, odd = first + third, second + fourth
        target[energy % half, 0] = even + odd
        target[energy % half, 1] = even - odd
        target[energy % half, 2] = first - third
        target[energy % half, 3] = second - fourth


def fold(block, pair):
    energies, moments, _, rows, columns = block.shape
    half = (energies // 2, moments, rows, columns)
    vmem = pl.BlockSpec(half, lambda i: (0, 0, 0, 0))
    return pl.pallas_call(
        fold_kernel,
        grid=(1,),
        in_specs=[
            pl.BlockSpec((energies, moments, None, rows, columns), lambda i: (0, 0, pair, 0, 0))
        ],
        out_specs=[vmem, vmem],
        out_shape=[jax.ShapeDtypeStruct(half, jnp.float32)] * 2,
        compiler_params=LIMIT,
        cost_estimate=pl.CostEstimate(flops=1000000, bytes_accessed=4000000, transcendentals=0),
        name="fold",
    )(block)


def mix_kernel(split, pair, place, shifts, weights, left_ref, right_ref, *rest):
    if split:
        *quarters, kept_ref, away_ref, window, out_ref = rest
    else:
        *quarters, result, window, out_ref, sems = rest
    quarter = quarters[0].shape[0]
    targets = quarter * (len(quarters) - 2)
    for spot, part in enumerate(quarters):
        for energy in range(quarter):
            window[spot * quarter + energy] = part[energy]
    factors = []
    for mode in range(NMODE):
        for side in range(2):
            w0, w1, w2, w3 = (weights[side, mode, moment] for moment in range(4))
            even, odd = w0 + w2, w1 + w3
            factors.append(
                ((even + odd) * 0.25, (even - odd) * 0.25, (w0 - w2) * 0.5, (w1 - w3) * 0.5)
            )
    rows = window.shape[2]

    def one_energy(energy, carry):
        stacked = [[] for _ in range(4)]
        for mode in range(NMODE):
            shift = shifts[mode]
            parts = []
            for side, spot in ((0, energy + quarter - shift), (1, energy + quarter + shift)):
                p, q, r, s = factors[2 * mode + side]
                total, swing, d0, d1 = (window[spot, part] for part in range(4))
                parts.append((p * total, q * swing, r * d0 - s * d1, s * d0 + r * d1))
            mixed = jnp.concatenate([a + b for a, b in zip(*parts)], axis=0)
            coarse = mixed.astype(jnp.bfloat16)
            fine = (mixed - coarse.astype(jnp.float32)).astype(jnp.bfloat16)
            right = right_ref[pair, mode].reshape(2 * right_ref.shape[3], right_ref.shape[4])
            product = jnp.dot(
                jnp.concatenate([coarse, fine], axis=1), right, preferred_element_type=jnp.float32
            )
            coarse = product.astype(jnp.bfloat16)
            fine = (product - coarse.astype(jnp.float32)).astype(jnp.bfloat16)
            for part in range(4):
                block = slice(part * rows, (part + 1) * rows)
                stacked[part] += [coarse[block], fine[block]]
        columns = jnp.concatenate([jnp.concatenate(pieces, axis=0) for pieces in stacked], axis=1)
        total = jnp.dot(left_ref[pair], columns, preferred_element_type=jnp.float32)
        width = out_ref.shape[-1]
        plain, swing, v0, v1 = (total[:, part * width : (part + 1) * width] for part in range(4))
        even, odd = plain + swing, plain - swing
        for moment, value in enumerate((even + v0, odd + v1, even - v0, odd - v1)):
            if split:
                away = jnp.where(lax.rem(energy, 2) == place[0], 0, 1)
                out_ref[away, energy // 2, moment] = value
            else:
                out_ref[energy, moment] = value
        if not split:
            pltpu.make_async_copy(out_ref.at[energy], result.at[energy], sems.at[energy]).start()
        return carry

    lax.fori_loop(0, targets, one_energy, 0, unroll=targets)
    if not split:
        for energy in range(targets):
            pltpu.make_async_copy(out_ref.at[energy], result.at[energy], sems.at[energy]).wait()
    if split:
        for x in range(kept_ref.shape[0]):
            kept_ref[x] = out_ref[0, x]
            away_ref[x] = out_ref[1, x]


def mix(split, place, shifts, weights, quarters, left, right, pair):
    quarter, moments, rows, columns = quarters[0].shape
    targets = quarter * (len(quarters) - 2)
    vmem = pl.BlockSpec(memory_space=pltpu.VMEM)
    smem = pl.BlockSpec(memory_space=pltpu.SMEM)
    scratch = [pltpu.VMEM((quarter * len(quarters), moments, rows, columns), jnp.float32)]
    if split:
        shape, outs = (targets // 2, moments, rows, columns), [vmem, vmem]
        scratch += [pltpu.VMEM((2, *shape), jnp.float32)]
    else:
        shape, outs = (targets, moments, rows, columns), [pl.BlockSpec(memory_space=pl.ANY)]
        scratch += [pltpu.VMEM(shape, jnp.float32), pltpu.SemaphoreType.DMA((targets,))]
    return pl.pallas_call(
        functools.partial(mix_kernel, split, pair),
        in_specs=[smem] * 3 + [vmem] * (2 + len(quarters)),
        out_specs=outs,
        out_shape=[jax.ShapeDtypeStruct(shape, jnp.float32) for _ in outs],
        scratch_shapes=scratch,
        compiler_params=LIMIT,
        cost_estimate=pl.CostEstimate(flops=2500000000, bytes_accessed=2000000, transcendentals=0),
        name="mix",
    )(place, shifts, weights, left, right, *quarters)


def sort_kernel(place, kept_low, kept_high, received_low, received_high, *targets):
    core, first = place[0], place[1]
    half = kept_low.shape[0]
    whole = targets[-1]
    targets = targets[:-1]
    for side, pieces in enumerate(((kept_low, kept_high), (received_low, received_high))):
        for x in range(2 * half):
            whole[side, x] = pieces[x // half][x % half]
    for step, target in enumerate(targets):
        where = lax.rem(first + step, 4)
        for other in range(4):
            x = jnp.where(core == 0, other, where)
            moment = jnp.where(core == 0, where, other)
            target[core, other] = whole[0, x, moment]
            target[1 - core, other] = whole[1, x, moment]


def turn_kernel(place, *refs):
    sources, targets = refs[:4], refs[4:]
    for step, target in enumerate(targets):
        column = lax.rem(place[2] + step, 4)
        for behind, source in enumerate(sources):
            for owner in range(2):
                target[behind, owner] = source[owner, column]


def move(kernel, place, arrays, shape, scratch=()):
    vmem = pl.BlockSpec(memory_space=pltpu.VMEM)
    return list(
        pl.pallas_call(
            kernel,
            in_specs=[pl.BlockSpec(memory_space=pltpu.SMEM)] + [vmem] * len(arrays),
            out_specs=[vmem] * 4,
            out_shape=[jax.ShapeDtypeStruct(shape, jnp.float32)] * 4,
            scratch_shapes=scratch,
            compiler_params=LIMIT,
            cost_estimate=pl.CostEstimate(flops=1000000, bytes_accessed=2000000, transcendentals=0),
        )(place, *arrays)
    )


def place_kernel(place, held, *rest):
    sources, (out, sems) = rest[:4], rest[4:]
    core, first, second = place[0], place[1], place[2]
    copies = []
    for step, source in enumerate(sources):
        along_second = lax.rem(second + 4 - step, 4)
        for behind in range(4):
            along_first = lax.rem(first + 4 - behind, 4)
            x = jnp.where(core == 0, along_second, along_first)
            y = jnp.where(core == 0, along_first, along_second)
            copies.append(
                pltpu.make_async_copy(
                    source.at[behind], out.at[x, :, y, 0], sems.at[step, behind]
                )
            )
    for copy in copies:
        copy.start()
    for copy in copies:
        copy.wait()


def fill_kernel(back, out, sem):
    copy = pltpu.make_async_copy(back, out.at[:, :, :, 1], sem.at[0])
    copy.start()
    copy.wait()


def put(place, landed, back):
    rows, columns = back.shape[1:]
    hbm = pl.BlockSpec(memory_space=pl.ANY)
    result = jax.ShapeDtypeStruct((4, 2, 4, 2, rows, columns), jnp.float32)
    cost = pl.CostEstimate(flops=1000000, bytes_accessed=4000000, transcendentals=0)
    half = pl.pallas_call(
        fill_kernel,
        in_specs=[hbm],
        out_specs=hbm,
        out_shape=result,
        scratch_shapes=[pltpu.SemaphoreType.DMA((1,))],
        compiler_params=LIMIT,
        cost_estimate=cost,
        name="fill",
    )(back.reshape(4, 2, 4, rows, columns))
    return pl.pallas_call(
        place_kernel,
        in_specs=[pl.BlockSpec(memory_space=pltpu.SMEM)] + [hbm] * 5,
        out_specs=hbm,
        out_shape=result,
        scratch_shapes=[pltpu.SemaphoreType.DMA((4, 4))],
        input_output_aliases={1: 0},
        compiler_params=LIMIT,
        cost_estimate=cost,
        name="place",
    )(place, half, *landed)


def ring(fn):
    sizes = [lax.axis_size(axis) for axis in AXES]
    pairs = []
    for z, x, c, y in itertools.product(*map(range, sizes)):
        tx, tc, ty = fn(x, c, y)
        pairs.append((((z * sizes[1] + x) * sizes[2] + c) * sizes[3] + y,
                      ((z * sizes[1] + tx % 4) * sizes[2] + tc) * sizes[3] + ty % 4))
    return pairs


def along(step, core):
    return ring(lambda x, c, y: (x, c, y + step) if c == core else (x + step, c, y))


def on_device(green_less, couplings, pair_atoms, shift_idx, weights):
    pairs, rows, columns = green_less.shape[2:]
    group = lax.axis_size(GROUP)
    moments = lax.axis_size("y")
    planes = lax.axis_size("z")
    here = lax.axis_index(GROUP)
    up = [(plane, plane + 1) for plane in range(planes - 1)]
    down = [(plane + 1, plane) for plane in range(planes - 1)]
    owned = pairs // group
    atoms = lax.dynamic_slice_in_dim(pair_atoms, here * owned, owned, 0)
    couplings = pltpu.with_memory_space_constraint(couplings, pltpu.HBM)
    x, c, y = (lax.axis_index(axis) for axis in GROUP)
    first, second = jnp.where(c == 0, y, x), jnp.where(c == 0, x, y)
    place = jnp.stack([c, first, second]).astype(jnp.int32)
    left, right = tables(atoms, couplings)
    moved = lax.all_to_all(
        green_less.reshape(group, owned, rows, columns), GROUP, 0, 0, tiled=True
    )
    block = moved.reshape(group // moments, moments, owned, rows, columns)
    halves = []
    for pair in range(owned):
        low, high = fold(block, pair)
        below = lax.ppermute(high, "z", up)
        above = lax.ppermute(low, "z", down)
        halves.append((below, low, high, above))

    def compute(split, pair, first_quarter, count):
        quarters = halves[pair][first_quarter : first_quarter + count]
        return mix(split, place, shift_idx, weights, quarters, left, right, pair)

    kept, received = [], []
    for upper in range(2):
        stay, away = compute(True, 0, upper, 3)
        received.append(lax.ppermute(away, AXES, ring(lambda x, c, y: (x, 1 - c, y))))
        kept.append(stay)
    arrived = move(
        sort_kernel,
        place,
        (*kept, *received),
        (2, 4, rows, columns),
        [pltpu.VMEM((2, 4, 4, rows, columns), jnp.float32)],
    )
    for step in (2, 1, 3):
        arrived[step] = lax.ppermute(arrived[step], AXES, along(step, 0))
    (result,) = compute(False, 1, 0, 4)
    back = lax.all_to_all(result.reshape(group, rows, columns), GROUP, 0, 0, tiled=True)
    landed = move(turn_kernel, place, arrived, (4, 2, rows, columns))
    for step in (2, 1, 3):
        landed[step] = lax.ppermute(landed[step], AXES, along(step, 1))
    return put(place, landed, back).reshape(green_less.shape)


def solution(mesh):
    sizes = dict(mesh.shape)
    chips = sizes["energy"] // 8
    split = Mesh(
        mesh.devices.reshape(chips, 4, 2, sizes["mom"]), ("z", "x", "c", "y")
    )
    placed = P("y", ("z", "x", "c"), None, None, None)

    return jax.shard_map(
        on_device,
        mesh=split,
        in_specs=(placed, P(), P(), P(), P()),
        out_specs=placed,
        check_vma=False,
    )
```

```python
import functools
import itertools

import jax
import jax.numpy as jnp
from jax import lax
from jax.experimental import pallas as pl
from jax.experimental.pallas import tpu as pltpu
from jax.sharding import Mesh
from jax.sharding import PartitionSpec as P

NMODE = 3
VMEM_BYTES = 16 * 2**20
LIMIT = pltpu.CompilerParams(vmem_limit_bytes=VMEM_BYTES)
GROUP = ("x", "c", "y")
AXES = ("z", "x", "c", "y")


def tables_kernel(atoms, coupling_hbm, left_ref, right_ref, picked, sems):
    pairs = left_ref.shape[0]
    copies = []
    for pair in range(pairs):
        for side in range(2):
            copy = pltpu.make_async_copy(
                coupling_hbm.at[atoms[pair, side]], picked.at[pair, side], sems.at[pair, side]
            )
            copy.start()
            copies.append(copy)
    for copy in copies:
        copy.wait()
    size = picked.shape[-1]
    nothing = jnp.zeros((size, size), jnp.float32)
    for pair in range(pairs):
        lefts = []
        for mode in range(NMODE):
            left = picked[pair, 0, mode].astype(jnp.float32)
            lefts += [left, left]
            turned = picked[pair, 1, mode].astype(jnp.float32).T
            upper = jnp.concatenate([turned, nothing], axis=1)
            lower = jnp.concatenate([nothing, turned], axis=1)
            both = jnp.concatenate([upper, lower], axis=0).astype(jnp.bfloat16)
            right_ref[pair, mode, 0] = both
            right_ref[pair, mode, 1] = both
        left_ref[pair] = jnp.concatenate(lefts, axis=1).astype(jnp.bfloat16)


def tables(atoms, couplings):
    pairs, size = atoms.shape[0], couplings.shape[-1]
    return pl.pallas_call(
        tables_kernel,
        grid_spec=pltpu.PrefetchScalarGridSpec(
            num_scalar_prefetch=1,
            grid=(1,),
            in_specs=[pl.BlockSpec(memory_space=pl.ANY)],
            out_specs=[
                pl.BlockSpec((pairs, size, 2 * NMODE * size), lambda i, a: (0, 0, 0)),
                pl.BlockSpec((pairs, NMODE, 2, 2 * size, 2 * size), lambda i, a: (0, 0, 0, 0, 0)),
            ],
            scratch_shapes=[
                pltpu.VMEM((pairs, 2, NMODE, size, size), jnp.bfloat16),
                pltpu.SemaphoreType.DMA((pairs, 2)),
            ],
        ),
        out_shape=[
            jax.ShapeDtypeStruct((pairs, size, 2 * NMODE * size), jnp.bfloat16),
            jax.ShapeDtypeStruct((pairs, NMODE, 2, 2 * size, 2 * size), jnp.bfloat16),
        ],
        compiler_params=LIMIT,
        cost_estimate=pl.CostEstimate(flops=1000000, bytes_accessed=4000000, transcendentals=0),
        name="tables",
    )(atoms, couplings)


def fold_kernel(block_ref, low_ref, high_ref):
    half = low_ref.shape[0]
    for energy in range(2 * half):
        target = low_ref if energy < half else high_ref
        first, second, third, fourth = (block_ref[energy, moment] for moment in range(4))
        even, odd = first + third, second + fourth
        target[energy % half, 0] = even + odd
        target[energy % half, 1] = even - odd
        target[energy % half, 2] = first - third
        target[energy % half, 3] = second - fourth


def fold(block, pair):
    energies, moments, _, rows, columns = block.shape
    half = (energies // 2, moments, rows, columns)
    vmem = pl.BlockSpec(half, lambda i: (0, 0, 0, 0))
    return pl.pallas_call(
        fold_kernel,
        grid=(1,),
        in_specs=[
            pl.BlockSpec((energies, moments, None, rows, columns), lambda i: (0, 0, pair, 0, 0))
        ],
        out_specs=[vmem, vmem],
        out_shape=[jax.ShapeDtypeStruct(half, jnp.float32)] * 2,
        compiler_params=LIMIT,
        cost_estimate=pl.CostEstimate(flops=1000000, bytes_accessed=4000000, transcendentals=0),
        name="fold",
    )(block)


def mix_kernel(split, pair, place, shifts, weights, left_ref, right_ref, *rest):
    if split:
        *quarters, kept_ref, away_ref, window, out_ref = rest
    else:
        *quarters, result, window, out_ref, sems = rest
    quarter = quarters[0].shape[0]
    targets = quarter * (len(quarters) - 2)
    for spot, part in enumerate(quarters):
        for energy in range(quarter):
            window[spot * quarter + energy] = part[energy]
    factors = []
    for mode in range(NMODE):
        for side in range(2):
            w0, w1, w2, w3 = (weights[side, mode, moment] for moment in range(4))
            even, odd = w0 + w2, w1 + w3
            factors.append(
                ((even + odd) * 0.25, (even - odd) * 0.25, (w0 - w2) * 0.5, (w1 - w3) * 0.5)
            )
    rows = window.shape[2]

    def one_energy(energy, carry):
        stacked = [[] for _ in range(4)]
        for mode in range(NMODE):
            shift = shifts[mode]
            parts = []
            for side, spot in ((0, energy + quarter - shift), (1, energy + quarter + shift)):
                p, q, r, s = factors[2 * mode + side]
                total, swing, d0, d1 = (window[spot, part] for part in range(4))
                parts.append((p * total, q * swing, r * d0 - s * d1, s * d0 + r * d1))
            mixed = jnp.concatenate([a + b for a, b in zip(*parts)], axis=0)
            coarse = mixed.astype(jnp.bfloat16)
            fine = (mixed - coarse.astype(jnp.float32)).astype(jnp.bfloat16)
            right = right_ref[pair, mode].reshape(2 * right_ref.shape[3], right_ref.shape[4])
            product = jnp.dot(
                jnp.concatenate([coarse, fine], axis=1), right, preferred_element_type=jnp.float32
            )
            coarse = product.astype(jnp.bfloat16)
            fine = (product - coarse.astype(jnp.float32)).astype(jnp.bfloat16)
            for part in range(4):
                block = slice(part * rows, (part + 1) * rows)
                stacked[part] += [coarse[block], fine[block]]
        columns = jnp.concatenate([jnp.concatenate(pieces, axis=0) for pieces in stacked], axis=1)
        total = jnp.dot(left_ref[pair], columns, preferred_element_type=jnp.float32)
        width = out_ref.shape[-1]
        plain, swing, v0, v1 = (total[:, part * width : (part + 1) * width] for part in range(4))
        even, odd = plain + swing, plain - swing
        for moment, value in enumerate((even + v0, odd + v1, even - v0, odd - v1)):
            if split:
                away = jnp.where(lax.rem(energy, 2) == place[0], 0, 1)
                out_ref[away, energy // 2, moment] = value
            else:
                out_ref[energy, moment] = value
        if not split:
            pltpu.make_async_copy(out_ref.at[energy], result.at[energy], sems.at[energy]).start()
        return carry

    lax.fori_loop(0, targets, one_energy, 0, unroll=targets)
    if not split:
        for energy in range(targets):
            pltpu.make_async_copy(out_ref.at[energy], result.at[energy], sems.at[energy]).wait()
    if split:
        for x in range(kept_ref.shape[0]):
            kept_ref[x] = out_ref[0, x]
            away_ref[x] = out_ref[1, x]


def mix(split, place, shifts, weights, quarters, left, right, pair):
    quarter, moments, rows, columns = quarters[0].shape
    targets = quarter * (len(quarters) - 2)
    vmem = pl.BlockSpec(memory_space=pltpu.VMEM)
    smem = pl.BlockSpec(memory_space=pltpu.SMEM)
    scratch = [pltpu.VMEM((quarter * len(quarters), moments, rows, columns), jnp.float32)]
    if split:
        shape, outs = (targets // 2, moments, rows, columns), [vmem, vmem]
        scratch += [pltpu.VMEM((2, *shape), jnp.float32)]
    else:
        shape, outs = (targets, moments, rows, columns), [pl.BlockSpec(memory_space=pl.ANY)]
        scratch += [pltpu.VMEM(shape, jnp.float32), pltpu.SemaphoreType.DMA((targets,))]
    return pl.pallas_call(
        functools.partial(mix_kernel, split, pair),
        in_specs=[smem] * 3 + [vmem] * (2 + len(quarters)),
        out_specs=outs,
        out_shape=[jax.ShapeDtypeStruct(shape, jnp.float32) for _ in outs],
        scratch_shapes=scratch,
        compiler_params=LIMIT,
        cost_estimate=pl.CostEstimate(flops=2500000000, bytes_accessed=2000000, transcendentals=0),
        name="mix",
    )(place, shifts, weights, left, right, *quarters)


def sort_kernel(place, kept_low, kept_high, received_low, received_high, *targets):
    core, first = place[0], place[1]
    half = kept_low.shape[0]

    def pick(low, high, x, moment):
        row = lax.rem(x, half)
        return jnp.where(x < half, low[row, moment], high[row, moment])

    for step, target in enumerate(targets):
        where = lax.rem(first + step, 4)
        for other in range(4):
            x = jnp.where(core == 0, other, where)
            moment = jnp.where(core == 0, where, other)
            target[core, other] = pick(kept_low, kept_high, x, moment)
            target[1 - core, other] = pick(received_low, received_high, x, moment)


def turn_kernel(place, *refs):
    sources, targets = refs[:4], refs[4:]
    for step, target in enumerate(targets):
        column = lax.rem(place[2] + step, 4)
        for behind, source in enumerate(sources):
            for owner in range(2):
                target[behind, owner] = source[owner, column]


def move(kernel, place, arrays, shape, scratch=()):
    vmem = pl.BlockSpec(memory_space=pltpu.VMEM)
    return list(
        pl.pallas_call(
            kernel,
            in_specs=[pl.BlockSpec(memory_space=pltpu.SMEM)] + [vmem] * len(arrays),
            out_specs=[vmem] * 4,
            out_shape=[jax.ShapeDtypeStruct(shape, jnp.float32)] * 4,
            scratch_shapes=scratch,
            compiler_params=LIMIT,
            cost_estimate=pl.CostEstimate(flops=1000000, bytes_accessed=2000000, transcendentals=0),
        )(place, *arrays)
    )


def place_kernel(place, held, *rest):
    sources, (out, sems) = rest[:4], rest[4:]
    core, first, second = place[0], place[1], place[2]
    copies = []
    for step, source in enumerate(sources):
        along_second = lax.rem(second + 4 - step, 4)
        for behind in range(4):
            along_first = lax.rem(first + 4 - behind, 4)
            x = jnp.where(core == 0, along_second, along_first)
            y = jnp.where(core == 0, along_first, along_second)
            copies.append(
                pltpu.make_async_copy(
                    source.at[behind], out.at[x, :, y, 0], sems.at[step, behind]
                )
            )
    for copy in copies:
        copy.start()
    for copy in copies:
        copy.wait()


def fill_kernel(back, out, sem):
    copy = pltpu.make_async_copy(back, out.at[:, :, :, 1], sem.at[0])
    copy.start()
    copy.wait()


def put(place, landed, back):
    rows, columns = back.shape[1:]
    hbm = pl.BlockSpec(memory_space=pl.ANY)
    result = jax.ShapeDtypeStruct((4, 2, 4, 2, rows, columns), jnp.float32)
    cost = pl.CostEstimate(flops=1000000, bytes_accessed=4000000, transcendentals=0)
    half = pl.pallas_call(
        fill_kernel,
        in_specs=[hbm],
        out_specs=hbm,
        out_shape=result,
        scratch_shapes=[pltpu.SemaphoreType.DMA((1,))],
        compiler_params=LIMIT,
        cost_estimate=cost,
        name="fill",
    )(back.reshape(4, 2, 4, rows, columns))
    return pl.pallas_call(
        place_kernel,
        in_specs=[pl.BlockSpec(memory_space=pltpu.SMEM)] + [hbm] * 5,
        out_specs=hbm,
        out_shape=result,
        scratch_shapes=[pltpu.SemaphoreType.DMA((4, 4))],
        input_output_aliases={1: 0},
        compiler_params=LIMIT,
        cost_estimate=cost,
        name="place",
    )(place, half, *landed)


def ring(fn):
    sizes = [lax.axis_size(axis) for axis in AXES]
    pairs = []
    for z, x, c, y in itertools.product(*map(range, sizes)):
        tx, tc, ty = fn(x, c, y)
        pairs.append((((z * sizes[1] + x) * sizes[2] + c) * sizes[3] + y,
                      ((z * sizes[1] + tx % 4) * sizes[2] + tc) * sizes[3] + ty % 4))
    return pairs


def along(step, core):
    return ring(lambda x, c, y: (x, c, y + step) if c == core else (x + step, c, y))


def on_device(green_less, couplings, pair_atoms, shift_idx, weights):
    pairs, rows, columns = green_less.shape[2:]
    group = lax.axis_size(GROUP)
    moments = lax.axis_size("y")
    planes = lax.axis_size("z")
    here = lax.axis_index(GROUP)
    up = [(plane, plane + 1) for plane in range(planes - 1)]
    down = [(plane + 1, plane) for plane in range(planes - 1)]
    owned = pairs // group
    atoms = lax.dynamic_slice_in_dim(pair_atoms, here * owned, owned, 0)
    couplings = pltpu.with_memory_space_constraint(couplings, pltpu.HBM)
    x, c, y = (lax.axis_index(axis) for axis in GROUP)
    first, second = jnp.where(c == 0, y, x), jnp.where(c == 0, x, y)
    place = jnp.stack([c, first, second]).astype(jnp.int32)
    left, right = tables(atoms, couplings)
    moved = lax.all_to_all(
        green_less.reshape(group, owned, rows, columns), GROUP, 0, 0, tiled=True
    )
    block = moved.reshape(group // moments, moments, owned, rows, columns)
    halves = []
    for pair in range(owned):
        low, high = fold(block, pair)
        below = lax.ppermute(high, "z", up)
        above = lax.ppermute(low, "z", down)
        halves.append((below, low, high, above))

    def compute(split, pair, first_quarter, count):
        quarters = halves[pair][first_quarter : first_quarter + count]
        return mix(split, place, shift_idx, weights, quarters, left, right, pair)

    kept, received = [], []
    for upper in range(2):
        stay, away = compute(True, 0, upper, 3)
        received.append(lax.ppermute(away, AXES, ring(lambda x, c, y: (x, 1 - c, y))))
        kept.append(stay)
    arrived = move(sort_kernel, place, (*kept, *received), (2, 4, rows, columns))
    for step in (2, 1, 3):
        arrived[step] = lax.ppermute(arrived[step], AXES, along(step, 0))
    (result,) = compute(False, 1, 0, 4)
    back = lax.all_to_all(result.reshape(group, rows, columns), GROUP, 0, 0, tiled=True)
    landed = move(turn_kernel, place, arrived, (4, 2, rows, columns))
    for step in (2, 1, 3):
        landed[step] = lax.ppermute(landed[step], AXES, along(step, 1))
    return put(place, landed, back).reshape(green_less.shape)


def solution(mesh):
    sizes = dict(mesh.shape)
    chips = sizes["energy"] // 8
    split = Mesh(
        mesh.devices.reshape(chips, 4, 2, sizes["mom"]), ("z", "x", "c", "y")
    )
    placed = P("y", ("z", "x", "c"), None, None, None)

    return jax.shard_map(
        on_device,
        mesh=split,
        in_specs=(placed, P(), P(), P(), P()),
        out_specs=placed,
        check_vma=False,
    )
```
